32 devices in a mesh: group: 2 (over x), sec: 16 (over z, y, core).
Axes of the slice: x: 2, y: 2, z: 4, core: 2. Of those that a mesh axis runs over, the one named last changes fastest.
Arguments:
- patches: bfloat16 [32, 128, 128, 128], P(('group', 'sec')), parts along dimension 0, may hold values from -24 to 24
- pair_list: int32 [32, 64], P(('group', 'sec')), parts along dimension 0, may hold values from 0 to 127, as said below
- pair_count: int32 [32], P(('group', 'sec')), parts along dimension 0, may hold values from 0 to 64, as said below
- tissue: int32 [32, 128], P(('group', 'sec')), parts along dimension 0, may hold values 0 or 1
Outputs:
- pair_flow: float32 [32, 2, 64], P(('group', 'sec')), parts along dimension 0
- positions: float32 [32, 2, 128], P(('group', 'sec')), parts along dimension 0
The draws below stay inside these ranges and needn't reach their ends.
There are 2 independent parts, one for each index of `group`. The reference program is written for one: setup_inputs(seed, part) draws one part's arguments, and reference() takes and returns one part's arrays. A program takes and returns all parts, laid end to end along the dimension named above; each array names one. Nothing has to cross between parts.
Inputs may be any that keep to these rules, and one draw needn't show every extreme that they name: `pair_list`: the first pair_count[s] entries of row s are distinct patch indices; the other entries are 0. `pair_count`: some section other than the last has exactly 64 live slots; the last section has 0.
All inputs are finite; a program needn't handle non-finite values. No bound on the sum of `tissue` on one device may be relied on, other than what follows from the above.
Results may differ from the reference program's by a relative error of at most 0.0029.
Values may be sent and summed in bfloat16 or wider, within the bound.
A program may use at most 64 MiB of HBM per device.

```python
import jax
import jax.numpy as jnp
from jax import lax

PS = 128
GR = 8
ITERS = 3
P_SIZE = 128
LIST = 64
SEC = 16


def shift_image(image, down_by, right_by):
    return jnp.roll(jnp.roll(image, down_by, axis=0), right_by, axis=1)


def draw_patches(key, part):
    base_field = jax.random.normal(jax.random.fold_in(key, 1), (P_SIZE, PS, PS), jnp.float32)
    reach = 3 * PS // 8
    offsets = jax.random.randint(jax.random.fold_in(key, 2), (SEC, P_SIZE, 2), -reach, reach + 1)
    toward = jax.random.randint(jax.random.fold_in(key, 3), (SEC, P_SIZE), 0, 2)
    uneven = jax.random.uniform(jax.random.fold_in(key, 4), (SEC, P_SIZE), jnp.float32, 0.015, 0.045)
    noise_keys = jax.random.split(jax.random.fold_in(key, 5), SEC)
    moved_images = jax.vmap(shift_image)

    def advance(earlier, section_inputs):
        offset_pair, side_pick, spread, noise_key = section_inputs
        primary = moved_images(earlier, offset_pair[:, 0], offset_pair[:, 1])
        second = moved_images(earlier, offset_pair[:, 0] + side_pick, offset_pair[:, 1] + 1 - side_pick)
        noise_part = jax.random.normal(noise_key, (P_SIZE, PS, PS), jnp.float32)
        new_field = 0.5 * primary + (0.5 - spread)[:, None, None] * second + 0.7 * noise_part
        return (new_field, new_field)
    final_field, rest_fields = lax.scan(advance, base_field, (offsets[:-1], toward[:-1], uneven[:-1], noise_keys[:-1]))
    stacked = jnp.concatenate([base_field[None], rest_fields], axis=0)
    faint_order = jax.random.permutation(jax.random.fold_in(key, 7), P_SIZE)
    faint_scale = jnp.where(faint_order < P_SIZE // 4, 0.15, 1.0).astype(jnp.float32)
    stacked = stacked * faint_scale[None, :, None, None]
    return jnp.clip(stacked, -24.0, 24.0).astype(jnp.bfloat16)


def permute_one(subkey):
    return jax.random.permutation(subkey, P_SIZE)


def list_helper(key):
    lowest = max(1, LIST // 8)
    highest = min(LIST, max(2, LIST // 2))
    counts = jax.random.randint(jax.random.fold_in(key, 11), (SEC,), lowest, highest + 1)
    busiest = jax.random.randint(jax.random.fold_in(key, 12), (), 0, SEC - 1)
    section_index = jnp.arange(SEC)
    counts = jnp.where(section_index == busiest, LIST, counts)
    counts = jnp.where(section_index == SEC - 1, 0, counts)
    orders = jax.vmap(permute_one)(jax.random.split(jax.random.fold_in(key, 13), SEC))
    slot_index = jnp.arange(LIST)
    listing = jnp.where(slot_index[None, :] < counts[:, None], orders[:, :LIST], 0)
    return (listing.astype(jnp.int32), counts.astype(jnp.int32))


def draw_pair_list(key, part):
    listing, counts = list_helper(key)
    return listing


def draw_pair_count(key, part):
    listing, counts = list_helper(key)
    return counts


def set_ends(drawn, own_key, least, top_value):
    dims = drawn.shape
    index_at = [jax.random.randint(jax.random.fold_in(own_key, axis), (), 0, dims[axis]) for axis in range(len(dims))]
    drawn = drawn.at[tuple(index_at)].set(least)
    longest = dims.index(max(dims))
    index_at[longest] = (index_at[longest] + 1) % dims[longest]
    return drawn.at[tuple(index_at)].set(top_value)


def setup_inputs(seed: int = 0, part: int = 0) -> dict:
    splits = jax.random.split(jax.random.key(seed), 5)
    part_splits = jax.random.split(jax.random.fold_in(splits[4], part), 5)
    return {
        "patches": draw_patches(jax.random.fold_in(jax.random.fold_in(splits[4], part), 71), part),
        "pair_list": draw_pair_list(jax.random.fold_in(jax.random.fold_in(splits[4], part), 71), part),
        "pair_count": draw_pair_count(jax.random.fold_in(jax.random.fold_in(splits[4], part), 71), part),
        "tissue": set_ends((jax.random.randint(part_splits[3], (SEC, P_SIZE), 0, 2) < 1).astype(jnp.int32), jax.random.fold_in(part_splits[3], 1), 0, 1),
    }


spring_rate = 0.25
step_rate = 0.15


def dft_tables(length):
    index = jnp.arange(length, dtype=jnp.int32)
    product = (index[:, None] * index[None, :]) % length
    angle_grid = product.astype(jnp.float32) * (2.0 * jnp.pi / length)
    return jnp.cos(angle_grid).astype(jnp.bfloat16), jnp.sin(angle_grid).astype(jnp.bfloat16)


def right_mul(patch_block, dft_table):
    return jnp.einsum('lxy,yk->lxk', patch_block.astype(jnp.float32), dft_table.astype(jnp.float32), precision=lax.Precision.HIGHEST)


def left_mul(dft_table, patch_block):
    return jnp.einsum('kx,lxy->lky', dft_table.astype(jnp.float32), patch_block.astype(jnp.float32), precision=lax.Precision.HIGHEST)


def spectrum_pair(patch_block, cosine_table, sine_table):
    with_cos = right_mul(patch_block, cosine_table).astype(jnp.bfloat16)
    with_sin = right_mul(patch_block, sine_table).astype(jnp.bfloat16)
    real_part = (left_mul(cosine_table, with_cos) - left_mul(sine_table, with_sin)).astype(jnp.bfloat16)
    imag_part = (-(left_mul(cosine_table, with_sin) + left_mul(sine_table, with_cos))).astype(jnp.bfloat16)
    return real_part.astype(jnp.float32), imag_part.astype(jnp.float32)


def soft_peak(lower_block, upper_block, cosine_table, sine_table):
    lower_real, lower_imag = spectrum_pair(lower_block, cosine_table, sine_table)
    upper_real, upper_imag = spectrum_pair(upper_block, cosine_table, sine_table)
    cross_real = (lower_real * upper_real + lower_imag * upper_imag).astype(jnp.bfloat16)
    cross_imag = (lower_real * upper_imag - lower_imag * upper_real).astype(jnp.bfloat16)
    inner_real = (right_mul(cross_real, cosine_table) - right_mul(cross_imag, sine_table)).astype(jnp.bfloat16)
    inner_imag = (right_mul(cross_real, sine_table) + right_mul(cross_imag, cosine_table)).astype(jnp.bfloat16)
    raw_corr = left_mul(cosine_table, inner_real) - left_mul(sine_table, inner_imag)
    side_length = raw_corr.shape[-1]
    scores = raw_corr * (64.0 / float(side_length * side_length * side_length * side_length))
    weights = jax.nn.softmax(scores.reshape(raw_corr.shape[0], -1), axis=-1).reshape(raw_corr.shape)
    lag_values = ((jnp.arange(side_length) + side_length // 2) % side_length - side_length // 2).astype(jnp.float32)
    shift_rows = jnp.sum(jnp.sum(weights, axis=2) * lag_values[None, :], axis=1)
    shift_cols = jnp.sum(jnp.sum(weights, axis=1) * lag_values[None, :], axis=1)
    return jnp.stack([shift_rows, shift_cols])


def pad_axis(values, before, after, axis_pos):
    widths = [(0, 0)] * values.ndim
    widths[axis_pos % values.ndim] = (before, after)
    return jnp.pad(values, widths)


def plane_force(field_vals, stiffness, grid_rows):
    full_shape = field_vals.shape
    grid_cols = full_shape[-1] // grid_rows
    grid = field_vals.reshape(full_shape[:-1] + (grid_rows, grid_cols))
    stiff_grid = stiffness.reshape(stiffness.shape[:-1] + (1, grid_rows, grid_cols))
    along_cols = 0.5 * (stiff_grid[..., 1:] + stiff_grid[..., :-1]) * (grid[..., 1:] - grid[..., :-1])
    col_force = pad_axis(along_cols, 1, 0, -1) - pad_axis(along_cols, 0, 1, -1)
    along_rows = 0.5 * (stiff_grid[..., 1:, :] + stiff_grid[..., :-1, :]) * (grid[..., 1:, :] - grid[..., :-1, :])
    row_force = pad_axis(along_rows, 1, 0, -2) - pad_axis(along_rows, 0, 1, -2)
    return (col_force + row_force).reshape(full_shape)


def mesh_force(middle, upper, lower, here_field, below_field, stiffness, grid_rows):
    gap_here = upper - middle - here_field[..., 0:2, :]
    gap_below = middle - lower - below_field[..., 0:2, :]
    return plane_force(middle, stiffness, grid_rows) - here_field[..., 2:3, :] * gap_here + below_field[..., 2:3, :] * gap_below


def shift_up(values):
    return jnp.concatenate([values[1:], jnp.zeros_like(values[:1])], axis=0)


def shift_down(values):
    return jnp.concatenate([jnp.zeros_like(values[:1]), values[:-1]], axis=0)


def reference(patches, pair_list, pair_count, tissue):
    cosine_table, sine_table = dft_tables(PS)
    above_all = shift_up(patches)

    def per_section(section_items):
        own_patches, next_patches, listing, live_count = section_items
        valid_mask = (jnp.arange(LIST) < live_count).astype(jnp.float32)
        slot_flows = soft_peak(own_patches[listing], next_patches[listing], cosine_table, sine_table) * valid_mask[None, :]
        onehot = (listing[:, None] == jnp.arange(P_SIZE)[None, :]).astype(jnp.float32) * valid_mask[:, None]
        moved_flows = jnp.dot(slot_flows, onehot, precision=lax.Precision.HIGHEST)
        pair_field = jnp.concatenate([moved_flows, jnp.sum(onehot, axis=0)[None, :]], axis=0)
        return slot_flows, pair_field

    pair_flow, pair_field = lax.map(per_section, (patches, above_all, pair_list, pair_count))
    stiffness = spring_rate * (1.0 + 2.0 * tissue.astype(jnp.float32))
    positions = jnp.zeros((SEC, 2, P_SIZE), jnp.float32)
    below_field = shift_down(pair_field)
    for sweep_step in range(ITERS):
        force_now = mesh_force(positions, shift_up(positions), shift_down(positions), pair_field, below_field, stiffness, GR)
        positions = positions - step_rate * force_now
    return pair_flow, positions
```

```python
import functools

import jax
import jax.numpy as jnp
import numpy as np
from jax import lax
from jax.experimental import pallas as pl
from jax.experimental.pallas import tpu as pltpu
from jax.sharding import PartitionSpec as P

GR = 8
SPRING = 0.25
STEP = 0.15
CHUNK = 8
EARLY = 2
HALO = 3
MESH = pl.DeviceIdType.MESH
F32 = jnp.float32
BF16 = jnp.bfloat16
HIGH = lax.Precision.HIGHEST


def dft_tables(length):
    index = np.arange(length)
    angle = (index[:, None] * index[None, :] % length) * (2.0 * np.pi / length)
    c = np.cos(angle).astype(np.float32)
    s = np.sin(angle).astype(np.float32)
    right = np.concatenate([c, s], axis=1)
    left = np.block([[c, -s], [-s, -c]])
    inner = np.block([[c, s], [-s, c]])
    last = np.concatenate([c, -s], axis=1)
    return tuple(jnp.asarray(t.astype(jnp.bfloat16)) for t in (right, left, inner, last))


def dot(a, b):
    return jnp.dot(a, b, preferred_element_type=F32)


def dot_nt(a, b):
    return lax.dot_general(a, b, (((1,), (1,)), ((), ())), precision=HIGH, preferred_element_type=F32)


def stacked(both, a, b, side):
    ra = both[a * side : (a + 1) * side]
    rb = both[b * side : (b + 1) * side]
    top = jnp.concatenate([ra[:, :side], rb[:, :side]], axis=1)
    low = jnp.concatenate([ra[:, side:], rb[:, side:]], axis=1)
    return jnp.concatenate([top, low], axis=0)


def spectra(images, right, left):
    side = images[0].shape[0]
    rows = jnp.concatenate(images, axis=0)
    both = dot(rows, right).astype(BF16)
    return [dot(left, stacked(both, 2 * i, 2 * i + 1, side)) for i in range(len(images) // 2)]


def lane_roll(x, shift):
    return pltpu.roll(x, shift % x.shape[-1], x.ndim - 1)


def kernel(
    n,
    right_ref,
    left_ref,
    inner_ref,
    last_ref,
    list_s,
    list_v,
    count_s,
    tissue_ref,
    patches_any,
    flow_ref,
    pos_ref,
    patches,
    far_list_v,
    far_list_s,
    outgoing,
    incoming,
    lower_spec,
    peak_ref,
    mass_ref,
    moment_ref,
    packet,
    halo,
    load_sem,
    smem_sem,
    list_sems,
    send_sems,
    recv_sems,
    halo_send,
    halo_recv,
):
    me = lax.axis_index("sec")
    total, side, _ = patches.shape
    slots = list_s.shape[1]
    chunks = slots // CHUNK
    offsets = [d for d in range(-HALO, HALO + 1) if d != 0]

    load = pltpu.make_async_copy(patches_any.at[0], patches, load_sem)
    load.start()

    halo[...] = jnp.zeros_like(halo)
    peak_ref[...] = jnp.zeros_like(peak_ref)
    mass_ref[...] = jnp.ones_like(mass_ref)
    moment_ref[...] = jnp.zeros_like(moment_ref)

    barrier = pltpu.get_barrier_semaphore()
    for d in offsets:

        @pl.when((me + d >= 0) & (me + d < n))
        def _():
            pl.semaphore_signal(barrier, inc=1, device_id={"sec": me + d}, device_id_type=MESH)

    pl.semaphore_wait(barrier, jnp.minimum(me, HALO) + jnp.minimum(n - 1 - me, HALO))

    list_copy = pltpu.make_async_remote_copy(
        src_ref=list_v,
        dst_ref=far_list_v,
        send_sem=list_sems.at[0],
        recv_sem=list_sems.at[1],
        device_id={"sec": me + 1},
        device_id_type=MESH,
    )

    @pl.when(me < n - 1)
    def _():
        list_copy.start()

    load.wait()

    def lower_group(g, carry):
        images = [patches[list_s[0, g * CHUNK + j]] for j in range(CHUNK)]
        for i, spec in enumerate(spectra(images, right_ref[...], left_ref[...])):
            lower_spec[g * (CHUNK // 2) + i] = spec.astype(BF16)
        return carry

    lax.fori_loop(0, EARLY, lower_group, 0)

    def patch_copy(c):
        return pltpu.make_async_remote_copy(
            src_ref=outgoing.at[pl.ds(c * CHUNK, CHUNK)],
            dst_ref=incoming.at[pl.ds(c * CHUNK, CHUNK)],
            send_sem=send_sems.at[c],
            recv_sem=recv_sems.at[c],
            device_id={"sec": me - 1},
            device_id_type=MESH,
        )

    @pl.when(me > 0)
    def _():
        list_copy.wait_recv()
        to_smem = pltpu.make_async_copy(far_list_v, far_list_s, smem_sem)
        to_smem.start()
        to_smem.wait()

        def gather(c):
            for j in range(CHUNK):
                outgoing[c * CHUNK + j] = patches[far_list_s[0, c * CHUNK + j]]

        gather(0)

        def send(c, carry):
            gather(c + 1)
            patch_copy(c).start()
            return carry

        lax.fori_loop(0, chunks - 1, send, 0)
        patch_copy(chunks - 1).start()

    lax.fori_loop(EARLY, chunks, lower_group, 0)

    half = side // 2
    row = lax.broadcasted_iota(jnp.int32, (side, 1), 0)
    row_lag = ((row + half) % side - half).astype(F32)
    scale = 64.0 / float(side * side * side * side)

    @pl.when(me < n - 1)
    def _():
        def upper_group(g, carry):
            patch_copy(g).wait_recv()
            images = [incoming[g * CHUNK + j] for j in range(CHUNK)]
            crosses = []
            for i, spec in enumerate(spectra(images, right_ref[...], left_ref[...])):
                ur = spec[:side].astype(BF16).astype(F32)
                ui = spec[side:].astype(BF16).astype(F32)
                low = lower_spec[g * (CHUNK // 2) + i].astype(F32)
                lr, li = low[:side], low[side:]
                cr = (lr * ur + li * ui).astype(BF16)
                ci = (lr * ui - li * ur).astype(BF16)
                crosses.append(jnp.concatenate([cr[:, :side], ci[:, :side]], axis=1))
                crosses.append(jnp.concatenate([cr[:, side:], ci[:, side:]], axis=1))
            inner = dot(jnp.concatenate(crosses, axis=0), inner_ref[...]).astype(BF16)
            peaks, masses, moments = [], [], []
            for i in range(CHUNK // 2):
                scores = dot(last_ref[...], stacked(inner, 2 * i, 2 * i + 1, side)) * scale
                peak = jnp.max(scores, axis=0, keepdims=True)
                e = jnp.exp(scores - peak)
                mass = jnp.sum(e, axis=0, keepdims=True)
                moment = jnp.sum(e * row_lag, axis=0, keepdims=True)
                for parts, value in ((peaks, peak), (masses, mass), (moments, moment)):
                    parts.append(value[:, :side])
                    parts.append(value[:, side:])
            at = pl.ds(pl.multiple_of(g * CHUNK, CHUNK), CHUNK)
            peak_ref[at, :] = jnp.concatenate(peaks, axis=0)
            mass_ref[at, :] = jnp.concatenate(masses, axis=0)
            moment_ref[at, :] = jnp.concatenate(moments, axis=0)
            return carry

        lax.fori_loop(0, chunks, upper_group, 0)

    peak = peak_ref[...]
    weight = jnp.exp(peak - jnp.max(peak, axis=1, keepdims=True))
    mass = mass_ref[...] * weight
    moment = moment_ref[...] * weight
    col = lax.broadcasted_iota(jnp.int32, (8, side), 1)
    sub = lax.broadcasted_iota(jnp.int32, (8, side), 0)
    col_lag = ((col + half) % side - half).astype(F32)
    probe = jnp.where(sub == 0, 1.0, jnp.where(sub == 1, col_lag, 0.0))
    sums = dot_nt(probe, mass)
    rows_num = dot_nt(probe, moment)
    mass_all = sums[0:1]
    live = lax.broadcasted_iota(jnp.int32, (1, slots), 1) < count_s[0]
    flow_rows = jnp.where(live, rows_num[0:1] / mass_all, 0.0)
    flow_cols = jnp.where(live, sums[1:2] / mass_all, 0.0)
    flow_ref[0] = jnp.concatenate([flow_rows, flow_cols], axis=0)
    which = lax.broadcasted_iota(jnp.int32, (total, slots), 0)
    onehot = (which == list_v[...]).astype(F32)
    stack = jnp.concatenate(
        [flow_rows, flow_cols, live.astype(F32), jnp.zeros((5, slots), F32)], axis=0
    )
    field = dot_nt(stack, onehot)
    sub_t = lax.broadcasted_iota(jnp.int32, (8, total), 0)
    packet[...] = jnp.where(sub_t == 3, tissue_ref[...].astype(F32), field)

    reach = [d for d in range(-HALO + 1, HALO + 1) if d != 0]

    def halo_copy(d):
        return pltpu.make_async_remote_copy(
            src_ref=packet,
            dst_ref=halo.at[HALO - d],
            send_sem=halo_send.at[HALO - d],
            recv_sem=halo_recv.at[HALO - d],
            device_id={"sec": me + d},
            device_id_type=MESH,
        )

    for d in reach:

        @pl.when((me + d >= 0) & (me + d < n))
        def _():
            halo_copy(d).start()

    for d in reach:

        @pl.when((me - d >= 0) & (me - d < n))
        def _():
            halo_copy(d).wait_recv()

    fields = {d: halo[HALO + d] for d in range(-HALO, HALO) if d != 0}
    fields[0] = packet[...]
    links = {d: jnp.broadcast_to(f[2:3], f.shape) for d, f in fields.items()}
    lane = lax.broadcasted_iota(jnp.int32, (8, total), 1)
    width = total // GR
    has_right = (lane % width) != width - 1
    has_below = lane < total - width

    def springs(d):
        tissue = jnp.broadcast_to(fields[d][3:4], (8, total))
        stiff = SPRING * (1.0 + 2.0 * tissue)
        across = jnp.where(has_right, 0.5 * (stiff + lane_roll(stiff, -1)), 0.0)
        along = jnp.where(has_below, 0.5 * (stiff + lane_roll(stiff, -width)), 0.0)
        return across, along

    def plane(u, spring):
        across, along = spring
        a = across * (lane_roll(u, -1) - u)
        b = along * (lane_roll(u, -width) - u)
        return (lane_roll(a, 1) - a) + (lane_roll(b, width) - b)

    spring = {d: springs(d) for d in (-1, 0, 1)}
    pull = {d: links[d] * fields[d] for d in fields}
    u1 = {d: -STEP * (pull[d] - pull[d - 1]) for d in range(-2, 3)}

    def relaxed(u, d):
        gap_here = u[d + 1] - u[d] - fields[d]
        gap_below = u[d] - u[d - 1] - fields[d - 1]
        force = plane(u[d], spring[d]) - links[d] * gap_here + links[d - 1] * gap_below
        return u[d] - STEP * force

    u2 = {d: relaxed(u1, d) for d in (-1, 0, 1)}
    pos_ref[0] = relaxed(u2, 0)[0:2]

    @pl.when(me < n - 1)
    def _():
        list_copy.wait_send()

    @pl.when(me > 0)
    def _():
        def drain(c, carry):
            patch_copy(c).wait_send()
            return carry

        lax.fori_loop(0, chunks, drain, 0)

    for d in reach:

        @pl.when((me + d >= 0) & (me + d < n))
        def _():
            halo_copy(d).wait_send()


def on_device(n, patches, pair_list, pair_count, tissue):
    _, total, side, _ = patches.shape
    slots = pair_list.shape[1]
    chunks = slots // CHUNK
    vmem = pl.BlockSpec(memory_space=pltpu.VMEM)
    smem = pl.BlockSpec(memory_space=pltpu.SMEM)
    dma = pltpu.SemaphoreType.DMA
    return pl.pallas_call(
        functools.partial(kernel, n),
        out_shape=(
            jax.ShapeDtypeStruct((1, 2, slots), F32),
            jax.ShapeDtypeStruct((1, 2, total), F32),
        ),
        in_specs=[vmem] * 4 + [smem, vmem, smem, vmem, pl.BlockSpec(memory_space=pl.ANY)],
        out_specs=(vmem, vmem),
        scratch_shapes=[
            pltpu.VMEM((total, side, side), BF16),
            pltpu.VMEM((1, slots), jnp.int32),
            pltpu.SMEM((1, slots), jnp.int32),
            pltpu.VMEM((slots, side, side), BF16),
            pltpu.VMEM((slots, side, side), BF16),
            pltpu.VMEM((slots // 2, 2 * side, 2 * side), BF16),
            pltpu.VMEM((slots, side), F32),
            pltpu.VMEM((slots, side), F32),
            pltpu.VMEM((slots, side), F32),
            pltpu.VMEM((8, total), F32),
            pltpu.VMEM((2 * HALO + 1, 8, total), F32),
            dma,
            dma,
            dma((2,)),
            dma((chunks,)),
            dma((chunks,)),
            dma((2 * HALO + 1,)),
            dma((2 * HALO + 1,)),
        ],
        compiler_params=pltpu.CompilerParams(
            collective_id=0, has_side_effects=True, vmem_limit_bytes=64_000_000
        ),
        name="section_match",
    )(*dft_tables(side), pair_list, pair_list, pair_count, tissue, patches)


def solution(mesh):
    return jax.shard_map(
        functools.partial(on_device, mesh.shape["sec"]),
        mesh=mesh,
        in_specs=(
            P(("group", "sec"), None, None, None),
            P(("group", "sec"), None),
            P(("group", "sec")),
            P(("group", "sec"), None),
        ),
        out_specs=(P(("group", "sec"), None, None), P(("group", "sec"), None, None)),
        check_vma=False,
    )
```

```python
import functools

import jax
import jax.numpy as jnp
import numpy as np
from jax import lax
from jax.experimental import pallas as pl
from jax.experimental.pallas import tpu as pltpu
from jax.sharding import PartitionSpec as P

GR = 8
SPRING = 0.25
STEP = 0.15
CHUNK = 8
HALO = 3
MESH = pl.DeviceIdType.MESH
F32 = jnp.float32
BF16 = jnp.bfloat16
HIGH = lax.Precision.HIGHEST


def dft_tables(length):
    index = np.arange(length)
    angle = (index[:, None] * index[None, :] % length) * (2.0 * np.pi / length)
    c = np.cos(angle).astype(np.float32)
    s = np.sin(angle).astype(np.float32)
    right = np.concatenate([c, s], axis=1)
    left = np.block([[c, -s], [-s, -c]])
    inner = np.block([[c, s], [-s, c]])
    last = np.concatenate([c, -s], axis=1)
    return tuple(jnp.asarray(t.astype(jnp.bfloat16)) for t in (right, left, inner, last))


def dot(a, b):
    return jnp.dot(a, b, preferred_element_type=F32)


def dot_nt(a, b):
    return lax.dot_general(a, b, (((1,), (1,)), ((), ())), precision=HIGH, preferred_element_type=F32)


def stacked(both, a, b, side):
    ra = both[a * side : (a + 1) * side]
    rb = both[b * side : (b + 1) * side]
    top = jnp.concatenate([ra[:, :side], rb[:, :side]], axis=1)
    low = jnp.concatenate([ra[:, side:], rb[:, side:]], axis=1)
    return jnp.concatenate([top, low], axis=0)


def spectra(images, right, left):
    side = images[0].shape[0]
    rows = jnp.concatenate(images, axis=0)
    both = dot(rows, right).astype(BF16)
    return [dot(left, stacked(both, 2 * i, 2 * i + 1, side)) for i in range(len(images) // 2)]


def lane_roll(x, shift):
    return pltpu.roll(x, shift % x.shape[-1], x.ndim - 1)


def up_chunks(pair, n, chunks):
    odd = pair % 2
    across = n // 2 - 1
    k = pair // 2
    return odd * (chunks * (k + 1) // (across + 1)) + (1 - odd) * (chunks // 2)


def exchange(
    n,
    right_any,
    left_any,
    inner_any,
    last_any,
    list_any,
    count_s,
    tissue_any,
    patches_any,
    out_ref,
    patches,
    right_ref,
    left_ref,
    inner_ref,
    last_ref,
    list_v,
    list_s,
    tissue_v,
    note,
    far_note,
    far_s,
    outgoing,
    incoming,
    own_spec,
    peak_ref,
    mass_ref,
    moment_ref,
    packet,
    halo,
    load_sems,
    smem_sem,
    list_sems,
    send_sems,
    recv_sems,
    halo_send,
    halo_recv,
):
    me = lax.axis_index("sec")
    total, side, _ = patches.shape
    slots = list_v.shape[1]
    chunks = slots // CHUNK
    offsets = [d for d in range(-HALO, HALO + 1) if d != 0]

    loads = [
        pltpu.make_async_copy(source, target, load_sems.at[i])
        for i, (source, target) in enumerate(
            (
                (list_any, list_v),
                (list_any, list_s),
                (patches_any.at[0], patches),
                (right_any, right_ref),
                (left_any, left_ref),
                (inner_any, inner_ref),
                (last_any, last_ref),
                (tissue_any, tissue_v),
            )
        )
    ]
    for load in loads:
        load.start()

    halo[...] = jnp.zeros_like(halo)
    far_note[...] = jnp.zeros_like(far_note)

    barrier = pltpu.get_barrier_semaphore()
    for d in offsets:

        @pl.when((me + d >= 0) & (me + d < n))
        def _():
            pl.semaphore_signal(barrier, inc=1, device_id={"sec": me + d}, device_id_type=MESH)

    peak_ref[...] = jnp.zeros_like(peak_ref)
    mass_ref[...] = jnp.ones_like(mass_ref)
    moment_ref[...] = jnp.zeros_like(moment_ref)
    for load in loads[:2]:
        load.wait()
    count = count_s[0]
    note[...] = jnp.concatenate([list_v[...], jnp.full((1, slots), count, jnp.int32)], axis=0)

    has_up = jnp.minimum(n - 1 - me, 1)
    has_down = jnp.minimum(me, 1)
    my_up = up_chunks(me, n, chunks)
    far_up = up_chunks(me - 1, n, chunks)

    pl.semaphore_wait(barrier, jnp.minimum(me, HALO) + jnp.minimum(n - 1 - me, HALO))

    list_copy = pltpu.make_async_remote_copy(
        src_ref=note,
        dst_ref=far_note,
        send_sem=list_sems.at[0],
        recv_sem=list_sems.at[1],
        device_id={"sec": me + 1},
        device_id_type=MESH,
    )

    @pl.when(me < n - 1)
    def _():
        list_copy.start()

    loads[2].wait()

    def patch_copy(q, to):
        return pltpu.make_async_remote_copy(
            src_ref=outgoing.at[pl.ds(q * CHUNK, CHUNK)],
            dst_ref=incoming.at[pl.ds(q * CHUNK, CHUNK)],
            send_sem=send_sems.at[q],
            recv_sem=recv_sems.at[q],
            device_id={"sec": to},
            device_id_type=MESH,
        )

    def send_up(c, carry):
        for j in range(CHUNK):
            outgoing[c * CHUNK + j] = patches[list_s[0, c * CHUNK + j]]
        patch_copy(c, me + 1).start()
        return carry

    lax.fori_loop(0, has_up * my_up, send_up, 0)
    for load in loads[3:]:
        load.wait()

    def own_group(q, carry):
        images = []
        for j in range(CHUNK):
            far = far_s[0, jnp.minimum(q, chunks - 1) * CHUNK + j]
            near = list_s[0, jnp.maximum(q - chunks, 0) * CHUNK + j]
            images.append(patches[jnp.where(q < chunks, far, near)])
        for i, spec in enumerate(spectra(images, right_ref[...], left_ref[...])):
            own_spec[q * (CHUNK // 2) + i] = spec.astype(BF16)
        return carry

    @pl.when(me > 0)
    def _():
        list_copy.wait_recv()

    to_smem = pltpu.make_async_copy(far_note, far_s, smem_sem)
    to_smem.start()
    to_smem.wait()

    def send_down(c, carry):
        for j in range(CHUNK):
            outgoing[slots + c * CHUNK + j] = patches[far_s[0, c * CHUNK + j]]
        patch_copy(chunks + c, me - 1).start()
        return carry

    lax.fori_loop(far_up, far_up + has_down * (chunks - far_up), send_down, 0)
    lax.fori_loop(chunks + my_up, chunks + my_up + has_up * (chunks - my_up), own_group, 0)
    lax.fori_loop(0, has_down * far_up, own_group, 0)

    half = side // 2
    row = lax.broadcasted_iota(jnp.int32, (side, 1), 0)
    row_lag = ((row + half) % side - half).astype(F32)
    scale = 64.0 / float(side * side * side * side)

    def match_group(t, carry):
        start_a, count_a, start_b = carry
        q = jnp.where(t < count_a, start_a + t, start_b + t - count_a)
        patch_copy(q, me).wait_recv()
        sign = jnp.where(q < chunks, -1.0, 1.0).astype(F32)
        images = [incoming[q * CHUNK + j] for j in range(CHUNK)]
        crosses = []
        for i, spec in enumerate(spectra(images, right_ref[...], left_ref[...])):
            ar = spec[:side].astype(BF16).astype(F32)
            ai = spec[side:].astype(BF16).astype(F32)
            own = own_spec[q * (CHUNK // 2) + i].astype(F32)
            br, bi = own[:side], own[side:]
            cr = (br * ar + bi * ai).astype(BF16)
            ci = ((br * ai - bi * ar) * sign).astype(BF16)
            crosses.append(jnp.concatenate([cr[:, :side], ci[:, :side]], axis=1))
            crosses.append(jnp.concatenate([cr[:, side:], ci[:, side:]], axis=1))
        inner = dot(jnp.concatenate(crosses, axis=0), inner_ref[...]).astype(BF16)
        peaks, masses, moments = [], [], []
        for i in range(CHUNK // 2):
            scores = dot(last_ref[...], stacked(inner, 2 * i, 2 * i + 1, side)) * scale
            peak = jnp.max(scores, axis=0, keepdims=True)
            e = jnp.exp(scores - peak)
            mass = jnp.sum(e, axis=0, keepdims=True)
            moment = jnp.sum(e * row_lag, axis=0, keepdims=True)
            for parts, value in ((peaks, peak), (masses, mass), (moments, moment)):
                parts.append(value[:, :side])
                parts.append(value[:, side:])
        at = pl.ds(pl.multiple_of(q * CHUNK, CHUNK), CHUNK)
        peak_ref[at, :] = jnp.concatenate(peaks, axis=0)
        mass_ref[at, :] = jnp.concatenate(masses, axis=0)
        moment_ref[at, :] = jnp.concatenate(moments, axis=0)
        return carry

    n_far = has_down * far_up
    n_near = has_up * (chunks - my_up)
    odd = me % 2
    start_a = (1 - odd) * (chunks + my_up)
    start_b = odd * (chunks + my_up)
    count_a = odd * n_far + (1 - odd) * n_near
    lax.fori_loop(0, n_far + n_near, match_group, (start_a, count_a, start_b))

    peak = peak_ref[...]
    weight = jnp.exp(peak - jnp.max(peak, axis=1, keepdims=True))
    mass = mass_ref[...] * weight
    moment = moment_ref[...] * weight
    col = lax.broadcasted_iota(jnp.int32, (8, side), 1)
    sub = lax.broadcasted_iota(jnp.int32, (8, side), 0)
    col_lag = ((col + half) % side - half).astype(F32)
    axes = jnp.where(sub == 0, 1.0, jnp.where(sub == 1, col_lag, 0.0))
    sums = dot_nt(axes, mass)
    rows_num = dot_nt(axes, moment)
    mass_all = sums[0:1]
    place = lax.broadcasted_iota(jnp.int32, (1, 2 * slots), 1)
    is_far = place < slots
    far = far_note[...]
    counts = jnp.concatenate([far[1:2], jnp.full((1, slots), count, jnp.int32)], axis=1)
    lists = jnp.concatenate([far[0:1], list_v[...]], axis=1)
    slot = jnp.where(is_far, place, place - slots)
    first = jnp.where(is_far, 0, (chunks - n_near) * CHUNK)
    stop = jnp.minimum(jnp.where(is_far, n_far * CHUNK, slots), counts)
    live = (slot >= first) & (slot < stop)
    flow_rows = jnp.where(live, rows_num[0:1] / mass_all, 0.0)
    flow_cols = jnp.where(live, sums[1:2] / mass_all, 0.0)
    which = lax.broadcasted_iota(jnp.int32, (total, 2 * slots), 0)
    onehot = (which == lists).astype(F32)
    one_pair = jnp.concatenate(
        [flow_rows, flow_cols, live.astype(F32), jnp.zeros((5, 2 * slots), F32)], axis=0
    )
    both = jnp.concatenate(
        [jnp.where(is_far, one_pair, 0.0), jnp.where(is_far, 0.0, one_pair)], axis=0
    )
    field = dot_nt(both, onehot)
    packet[0:3] = field[0:3]
    packet[3:4] = tissue_v[...].astype(F32)
    packet[4:8] = field[4:8]
    packet[8:16] = field[8:16]
    packet[4:5, 0 : 2 * slots] = flow_rows
    packet[5:6, 0 : 2 * slots] = flow_cols

    def halo_copy(d):
        return pltpu.make_async_remote_copy(
            src_ref=packet,
            dst_ref=halo.at[HALO - d],
            send_sem=halo_send.at[HALO - d],
            recv_sem=halo_recv.at[HALO - d],
            device_id={"sec": me + d},
            device_id_type=MESH,
        )

    for d in offsets:

        @pl.when((me + d >= 0) & (me + d < n))
        def _():
            halo_copy(d).start()

    @pl.when(me < n - 1)
    def _():
        list_copy.wait_send()

    def drain_up(c, carry):
        patch_copy(c, me + 1).wait_send()
        return carry

    lax.fori_loop(0, has_up * my_up, drain_up, 0)

    def drain_down(c, carry):
        patch_copy(chunks + c, me - 1).wait_send()
        return carry

    lax.fori_loop(far_up, far_up + has_down * (chunks - far_up), drain_down, 0)
    for d in offsets:

        @pl.when((me - d >= 0) & (me - d < n))
        def _():
            halo_copy(d).wait_recv()

    for d in offsets:
        out_ref[HALO + d] = halo[HALO + d]
    out_ref[HALO] = packet[...]
    for d in offsets:

        @pl.when((me + d >= 0) & (me + d < n))
        def _():
            halo_copy(d).wait_send()


def relax(halo, flow_ref, pos_ref):
    total = halo.shape[-1]
    slots = flow_ref.shape[-1]
    near, above = halo[HALO], halo[HALO + 1]
    flow_ref[0] = near[4:6, slots : 2 * slots] + above[4:6, 0:slots]
    fields = {d: halo[HALO + d][8:16] + halo[HALO + d + 1][0:8] for d in range(-HALO, HALO)}
    links = {d: jnp.broadcast_to(f[2:3], f.shape) for d, f in fields.items()}
    lane = lax.broadcasted_iota(jnp.int32, (8, total), 1)
    width = total // GR
    has_right = (lane % width) != width - 1
    has_below = lane < total - width

    def springs(d):
        tissue = jnp.broadcast_to(halo[HALO + d][3:4], (8, total))
        stiff = SPRING * (1.0 + 2.0 * tissue)
        across = jnp.where(has_right, 0.5 * (stiff + lane_roll(stiff, -1)), 0.0)
        along = jnp.where(has_below, 0.5 * (stiff + lane_roll(stiff, -width)), 0.0)
        return across, along

    def plane(u, spring):
        across, along = spring
        a = across * (lane_roll(u, -1) - u)
        b = along * (lane_roll(u, -width) - u)
        return (lane_roll(a, 1) - a) + (lane_roll(b, width) - b)

    spring = {d: springs(d) for d in (-1, 0, 1)}
    pull = {d: links[d] * fields[d] for d in fields}
    u1 = {d: -STEP * (pull[d] - pull[d - 1]) for d in range(-2, 3)}

    def relaxed(u, d):
        gap_here = u[d + 1] - u[d] - fields[d]
        gap_below = u[d] - u[d - 1] - fields[d - 1]
        force = plane(u[d], spring[d]) - links[d] * gap_here + links[d - 1] * gap_below
        return u[d] - STEP * force

    u2 = {d: relaxed(u1, d) for d in (-1, 0, 1)}
    pos_ref[0] = relaxed(u2, 0)[0:2]


def on_device(n, patches, pair_list, pair_count, tissue):
    _, total, side, _ = patches.shape
    slots = pair_list.shape[1]
    chunks = slots // CHUNK
    vmem = pl.BlockSpec(memory_space=pltpu.VMEM)
    any_space = pl.BlockSpec(memory_space=pl.ANY)
    dma = pltpu.SemaphoreType.DMA
    halo = pl.pallas_call(
        functools.partial(exchange, n),
        out_shape=jax.ShapeDtypeStruct((2 * HALO + 1, 16, total), F32),
        in_specs=[any_space] * 5 + [pl.BlockSpec(memory_space=pltpu.SMEM)] + [any_space] * 2,
        out_specs=vmem,
        scratch_shapes=[
            pltpu.VMEM((total, side, side), BF16),
            pltpu.VMEM((side, 2 * side), BF16),
            pltpu.VMEM((2 * side, 2 * side), BF16),
            pltpu.VMEM((2 * side, 2 * side), BF16),
            pltpu.VMEM((side, 2 * side), BF16),
            pltpu.VMEM((1, slots), jnp.int32),
            pltpu.SMEM((1, slots), jnp.int32),
            pltpu.VMEM((1, total), jnp.int32),
            pltpu.VMEM((2, slots), jnp.int32),
            pltpu.VMEM((2, slots), jnp.int32),
            pltpu.SMEM((2, slots), jnp.int32),
            pltpu.VMEM((2 * slots, side, side), BF16),
            pltpu.VMEM((2 * slots, side, side), BF16),
            pltpu.VMEM((slots, 2 * side, 2 * side), BF16),
            pltpu.VMEM((2 * slots, side), F32),
            pltpu.VMEM((2 * slots, side), F32),
            pltpu.VMEM((2 * slots, side), F32),
            pltpu.VMEM((16, total), F32),
            pltpu.VMEM((2 * HALO + 1, 16, total), F32),
            dma((8,)),
            dma,
            dma((2,)),
            dma((2 * chunks,)),
            dma((2 * chunks,)),
            dma((2 * HALO + 1,)),
            dma((2 * HALO + 1,)),
        ],
        compiler_params=pltpu.CompilerParams(
            collective_id=0, has_side_effects=True, vmem_limit_bytes=64_000_000
        ),
        name="exchange",
    )(*dft_tables(side), pair_list, pair_count, tissue, patches)
    return pl.pallas_call(
        relax,
        out_shape=(
            jax.ShapeDtypeStruct((1, 2, slots), F32),
            jax.ShapeDtypeStruct((1, 2, total), F32),
        ),
        in_specs=[vmem],
        out_specs=(vmem, vmem),
        name="relax",
    )(halo)


def solution(mesh):
    return jax.shard_map(
        functools.partial(on_device, mesh.shape["sec"]),
        mesh=mesh,
        in_specs=(
            P(("group", "sec"), None, None, None),
            P(("group", "sec"), None),
            P(("group", "sec")),
            P(("group", "sec"), None),
        ),
        out_specs=(P(("group", "sec"), None, None), P(("group", "sec"), None, None)),
        check_vma=False,
    )
```

```python
import functools

import jax
import jax.numpy as jnp
import numpy as np
from jax import lax
from jax.experimental import pallas as pl
from jax.experimental.pallas import tpu as pltpu
from jax.sharding import PartitionSpec as P

GR = 8
SPRING = 0.25
STEP = 0.15
CHUNK = 8
HALO = 3
MESH = pl.DeviceIdType.MESH
F32 = jnp.float32
BF16 = jnp.bfloat16


def dft_tables(length):
    index = np.arange(length)
    angle = (index[:, None] * index[None, :] % length) * (2.0 * np.pi / length)
    c = np.cos(angle).astype(np.float32)
    s = np.sin(angle).astype(np.float32)
    right = np.concatenate([c, s], axis=1)
    left = np.block([[c, -s], [-s, -c]])
    inner = np.block([[c, s], [-s, c]])
    last = np.concatenate([c, -s], axis=1)
    return tuple(jnp.asarray(t.astype(jnp.bfloat16)) for t in (right, left, inner, last))


def dot(a, b):
    return jnp.dot(a, b, preferred_element_type=F32)


def dot_nt(a, b):
    return lax.dot_general(a, b, (((1,), (1,)), ((), ())), preferred_element_type=F32)


def split3(x):
    top = x.astype(BF16)
    rest = x - top.astype(F32)
    mid = rest.astype(BF16)
    return top, mid, (rest - mid.astype(F32)).astype(BF16)


def stacked(both, a, b, side):
    ra = both[a * side : (a + 1) * side]
    rb = both[b * side : (b + 1) * side]
    top = jnp.concatenate([ra[:, :side], rb[:, :side]], axis=1)
    low = jnp.concatenate([ra[:, side:], rb[:, side:]], axis=1)
    return jnp.concatenate([top, low], axis=0)


def spectra(images, right, left):
    side = images[0].shape[0]
    rows = jnp.concatenate(images, axis=0)
    both = dot(rows, right).astype(BF16)
    return [dot(left, stacked(both, 2 * i, 2 * i + 1, side)) for i in range(len(images) // 2)]


def lane_roll(x, shift):
    return pltpu.roll(x, shift % x.shape[-1], x.ndim - 1)


def up_chunks(pair, n, chunks):
    return chunks * ((pair + 1) // 2) // (n // 2)


def exchange(
    n,
    right_any,
    left_any,
    inner_any,
    last_any,
    list_any,
    count_s,
    tissue_any,
    patches_any,
    out_ref,
    patches,
    right_ref,
    left_ref,
    inner_ref,
    last_ref,
    list_v,
    list_s,
    tissue_v,
    note,
    far_note,
    far_s,
    outgoing,
    incoming,
    own_spec,
    peak_ref,
    mass_ref,
    moment_ref,
    packet,
    halo,
    load_sems,
    smem_sem,
    list_sems,
    send_sems,
    recv_sems,
    halo_send,
    halo_recv,
):
    me = lax.axis_index("sec")
    total, side, _ = patches.shape
    slots = list_v.shape[1]
    chunks = slots // CHUNK
    offsets = [d for d in range(-HALO, HALO + 1) if d != 0]

    loads = [
        pltpu.make_async_copy(source, target, load_sems.at[i])
        for i, (source, target) in enumerate(
            (
                (list_any, list_v),
                (list_any, list_s),
                (patches_any.at[0], patches),
                (right_any, right_ref),
                (left_any, left_ref),
                (inner_any, inner_ref),
                (last_any, last_ref),
                (tissue_any, tissue_v),
            )
        )
    ]
    for load in loads:
        load.start()

    halo[...] = jnp.zeros_like(halo)
    far_note[...] = jnp.zeros_like(far_note)

    barrier = pltpu.get_barrier_semaphore()
    for d in offsets:

        @pl.when((me + d >= 0) & (me + d < n))
        def _():
            pl.semaphore_signal(barrier, inc=1, device_id={"sec": me + d}, device_id_type=MESH)

    peak_ref[...] = jnp.zeros_like(peak_ref)
    mass_ref[...] = jnp.ones_like(mass_ref)
    moment_ref[...] = jnp.zeros_like(moment_ref)
    for load in loads[:2]:
        load.wait()
    count = count_s[0]
    note[...] = jnp.concatenate([list_v[...], jnp.full((1, slots), count, jnp.int32)], axis=0)

    has_up = jnp.minimum(n - 1 - me, 1)
    has_down = jnp.minimum(me, 1)
    my_up = up_chunks(me, n, chunks)
    far_up = up_chunks(me - 1, n, chunks)

    pl.semaphore_wait(barrier, jnp.minimum(me, HALO) + jnp.minimum(n - 1 - me, HALO))

    list_copy = pltpu.make_async_remote_copy(
        src_ref=note,
        dst_ref=far_note,
        send_sem=list_sems.at[0],
        recv_sem=list_sems.at[1],
        device_id={"sec": me + 1},
        device_id_type=MESH,
    )

    @pl.when(me < n - 1)
    def _():
        list_copy.start()

    loads[2].wait()

    def patch_copy(q, to):
        return pltpu.make_async_remote_copy(
            src_ref=outgoing.at[pl.ds(q * CHUNK, CHUNK)],
            dst_ref=incoming.at[pl.ds(q * CHUNK, CHUNK)],
            send_sem=send_sems.at[q],
            recv_sem=recv_sems.at[q],
            device_id={"sec": to},
            device_id_type=MESH,
        )

    def send_up(c, carry):
        for j in range(CHUNK):
            outgoing[c * CHUNK + j] = patches[list_s[0, c * CHUNK + j]]
        patch_copy(c, me + 1).start()
        return carry

    lax.fori_loop(0, has_up * my_up, send_up, 0)
    for load in loads[3:]:
        load.wait()

    def own_group(q, carry):
        images = []
        for j in range(CHUNK):
            far = far_s[0, jnp.minimum(q, chunks - 1) * CHUNK + j]
            near = list_s[0, jnp.maximum(q - chunks, 0) * CHUNK + j]
            images.append(patches[jnp.where(q < chunks, far, near)])
        for i, spec in enumerate(spectra(images, right_ref[...], left_ref[...])):
            own_spec[q * (CHUNK // 2) + i] = spec.astype(BF16)
        return carry

    @pl.when(me > 0)
    def _():
        list_copy.wait_recv()

    to_smem = pltpu.make_async_copy(far_note, far_s, smem_sem)
    to_smem.start()
    to_smem.wait()

    def send_down(c, carry):
        for j in range(CHUNK):
            outgoing[slots + c * CHUNK + j] = patches[far_s[0, c * CHUNK + j]]
        patch_copy(chunks + c, me - 1).start()
        return carry

    lax.fori_loop(far_up, far_up + has_down * (chunks - far_up), send_down, 0)
    lax.fori_loop(chunks + my_up, chunks + my_up + has_up * (chunks - my_up), own_group, 0)
    lax.fori_loop(0, has_down * far_up, own_group, 0)

    half = side // 2
    row = lax.broadcasted_iota(jnp.int32, (side, 1), 0)
    row_lag = ((row + half) % side - half).astype(F32)
    scale = 64.0 / float(side * side * side * side)

    def match_group(t, carry):
        start_a, count_a, start_b = carry
        q = jnp.where(t < count_a, start_a + t, start_b + t - count_a)
        patch_copy(q, me).wait_recv()
        sign = jnp.where(q < chunks, -1.0, 1.0).astype(F32)
        images = [incoming[q * CHUNK + j] for j in range(CHUNK)]
        crosses = []
        for i, spec in enumerate(spectra(images, right_ref[...], left_ref[...])):
            ar = spec[:side].astype(BF16).astype(F32)
            ai = spec[side:].astype(BF16).astype(F32)
            own = own_spec[q * (CHUNK // 2) + i].astype(F32)
            br, bi = own[:side], own[side:]
            cr = (br * ar + bi * ai).astype(BF16)
            ci = ((br * ai - bi * ar) * sign).astype(BF16)
            crosses.append(jnp.concatenate([cr[:, :side], ci[:, :side]], axis=1))
            crosses.append(jnp.concatenate([cr[:, side:], ci[:, side:]], axis=1))
        inner = dot(jnp.concatenate(crosses, axis=0), inner_ref[...]).astype(BF16)
        peaks, masses, moments = [], [], []
        for i in range(CHUNK // 2):
            scores = dot(last_ref[...], stacked(inner, 2 * i, 2 * i + 1, side)) * scale
            peak = jnp.max(scores, axis=0, keepdims=True)
            e = jnp.exp(scores - peak)
            mass = jnp.sum(e, axis=0, keepdims=True)
            moment = jnp.sum(e * row_lag, axis=0, keepdims=True)
            for parts, value in ((peaks, peak), (masses, mass), (moments, moment)):
                parts.append(value[:, :side])
                parts.append(value[:, side:])
        at = pl.ds(pl.multiple_of(q * CHUNK, CHUNK), CHUNK)
        peak_ref[at, :] = jnp.concatenate(peaks, axis=0)
        mass_ref[at, :] = jnp.concatenate(masses, axis=0)
        moment_ref[at, :] = jnp.concatenate(moments, axis=0)
        return carry

    n_far = has_down * far_up
    n_near = has_up * (chunks - my_up)
    odd = me % 2
    start_a = (1 - odd) * (chunks + my_up)
    start_b = odd * (chunks + my_up)
    count_a = odd * n_far + (1 - odd) * n_near
    lax.fori_loop(0, n_far + n_near, match_group, (start_a, count_a, start_b))

    peak = peak_ref[...]
    weight = jnp.exp(peak - jnp.max(peak, axis=1, keepdims=True))
    mass = mass_ref[...] * weight
    moment = moment_ref[...] * weight
    col = lax.broadcasted_iota(jnp.int32, (8, side), 1)
    sub = lax.broadcasted_iota(jnp.int32, (8, side), 0)
    col_lag = ((col + half) % side - half).astype(F32)
    axes = jnp.where(sub == 0, 1.0, jnp.where(sub == 1, col_lag, 0.0))
    thirds = jnp.concatenate(split3(jnp.concatenate([mass, moment], axis=0)), axis=0)
    triple = dot_nt(axes.astype(BF16), thirds)
    span = 4 * slots
    joined = triple[:, 0:span] + triple[:, span : 2 * span] + triple[:, 2 * span :]
    sums, rows_num = joined[:, 0 : 2 * slots], joined[:, 2 * slots :]
    mass_all = sums[0:1]
    place = lax.broadcasted_iota(jnp.int32, (1, 2 * slots), 1)
    is_far = place < slots
    far = far_note[...]
    counts = jnp.concatenate([far[1:2], jnp.full((1, slots), count, jnp.int32)], axis=1)
    lists = jnp.concatenate([far[0:1], list_v[...]], axis=1)
    slot = jnp.where(is_far, place, place - slots)
    first = jnp.where(is_far, 0, (chunks - n_near) * CHUNK)
    stop = jnp.minimum(jnp.where(is_far, n_far * CHUNK, slots), counts)
    live = (slot >= first) & (slot < stop)
    flow_rows = jnp.where(live, rows_num[0:1] / mass_all, 0.0)
    flow_cols = jnp.where(live, sums[1:2] / mass_all, 0.0)
    which = lax.broadcasted_iota(jnp.int32, (total, 2 * slots), 0)
    onehot = (which == lists).astype(F32).astype(BF16)
    one_pair = jnp.concatenate(
        [flow_rows, flow_cols, live.astype(F32), jnp.zeros((5, 2 * slots), F32)], axis=0
    )
    both = jnp.concatenate(
        [jnp.where(is_far, one_pair, 0.0), jnp.where(is_far, 0.0, one_pair)], axis=0
    )
    triple = dot_nt(jnp.concatenate(split3(both), axis=0), onehot)
    field = triple[0:16] + triple[16:32] + triple[32:48]
    packet[0:3] = field[0:3]
    packet[3:4] = tissue_v[...].astype(F32)
    packet[4:8] = field[4:8]
    packet[8:16] = field[8:16]
    packet[4:5, 0 : 2 * slots] = flow_rows
    packet[5:6, 0 : 2 * slots] = flow_cols

    def halo_copy(d):
        return pltpu.make_async_remote_copy(
            src_ref=packet,
            dst_ref=halo.at[HALO - d],
            send_sem=halo_send.at[HALO - d],
            recv_sem=halo_recv.at[HALO - d],
            device_id={"sec": me + d},
            device_id_type=MESH,
        )

    for d in offsets:

        @pl.when((me + d >= 0) & (me + d < n))
        def _():
            halo_copy(d).start()

    @pl.when(me < n - 1)
    def _():
        list_copy.wait_send()

    def drain_up(c, carry):
        patch_copy(c, me + 1).wait_send()
        return carry

    lax.fori_loop(0, has_up * my_up, drain_up, 0)

    def drain_down(c, carry):
        patch_copy(chunks + c, me - 1).wait_send()
        return carry

    lax.fori_loop(far_up, far_up + has_down * (chunks - far_up), drain_down, 0)
    for d in offsets:

        @pl.when((me - d >= 0) & (me - d < n))
        def _():
            halo_copy(d).wait_recv()

    for d in offsets:
        out_ref[HALO + d] = halo[HALO + d]
    out_ref[HALO] = packet[...]
    for d in offsets:

        @pl.when((me + d >= 0) & (me + d < n))
        def _():
            halo_copy(d).wait_send()


def relax(halo, flow_ref, pos_ref):
    total = halo.shape[-1]
    slots = flow_ref.shape[-1]
    near, above = halo[HALO], halo[HALO + 1]
    flow_ref[0] = near[4:6, slots : 2 * slots] + above[4:6, 0:slots]
    fields = {d: halo[HALO + d][8:16] + halo[HALO + d + 1][0:8] for d in range(-HALO, HALO)}
    links = {d: jnp.broadcast_to(f[2:3], f.shape) for d, f in fields.items()}
    lane = lax.broadcasted_iota(jnp.int32, (8, total), 1)
    width = total // GR
    has_right = (lane % width) != width - 1
    has_below = lane < total - width

    def springs(d):
        tissue = jnp.broadcast_to(halo[HALO + d][3:4], (8, total))
        stiff = SPRING * (1.0 + 2.0 * tissue)
        across = jnp.where(has_right, 0.5 * (stiff + lane_roll(stiff, -1)), 0.0)
        along = jnp.where(has_below, 0.5 * (stiff + lane_roll(stiff, -width)), 0.0)
        return across, along

    def plane(u, spring):
        across, along = spring
        a = across * (lane_roll(u, -1) - u)
        b = along * (lane_roll(u, -width) - u)
        return (lane_roll(a, 1) - a) + (lane_roll(b, width) - b)

    spring = {d: springs(d) for d in (-1, 0, 1)}
    pull = {d: links[d] * fields[d] for d in fields}
    u1 = {d: -STEP * (pull[d] - pull[d - 1]) for d in range(-2, 3)}

    def relaxed(u, d):
        gap_here = u[d + 1] - u[d] - fields[d]
        gap_below = u[d] - u[d - 1] - fields[d - 1]
        force = plane(u[d], spring[d]) - links[d] * gap_here + links[d - 1] * gap_below
        return u[d] - STEP * force

    u2 = {d: relaxed(u1, d) for d in (-1, 0, 1)}
    pos_ref[0] = relaxed(u2, 0)[0:2]


def on_device(n, patches, pair_list, pair_count, tissue):
    _, total, side, _ = patches.shape
    slots = pair_list.shape[1]
    chunks = slots // CHUNK
    vmem = pl.BlockSpec(memory_space=pltpu.VMEM)
    any_space = pl.BlockSpec(memory_space=pl.ANY)
    dma = pltpu.SemaphoreType.DMA
    halo = pl.pallas_call(
        functools.partial(exchange, n),
        out_shape=jax.ShapeDtypeStruct((2 * HALO + 1, 16, total), F32),
        in_specs=[any_space] * 5 + [pl.BlockSpec(memory_space=pltpu.SMEM)] + [any_space] * 2,
        out_specs=vmem,
        scratch_shapes=[
            pltpu.VMEM((total, side, side), BF16),
            pltpu.VMEM((side, 2 * side), BF16),
            pltpu.VMEM((2 * side, 2 * side), BF16),
            pltpu.VMEM((2 * side, 2 * side), BF16),
            pltpu.VMEM((side, 2 * side), BF16),
            pltpu.VMEM((1, slots), jnp.int32),
            pltpu.SMEM((1, slots), jnp.int32),
            pltpu.VMEM((1, total), jnp.int32),
            pltpu.VMEM((2, slots), jnp.int32),
            pltpu.VMEM((2, slots), jnp.int32),
            pltpu.SMEM((2, slots), jnp.int32),
            pltpu.VMEM((2 * slots, side, side), BF16),
            pltpu.VMEM((2 * slots, side, side), BF16),
            pltpu.VMEM((slots, 2 * side, 2 * side), BF16),
            pltpu.VMEM((2 * slots, side), F32),
            pltpu.VMEM((2 * slots, side), F32),
            pltpu.VMEM((2 * slots, side), F32),
            pltpu.VMEM((16, total), F32),
            pltpu.VMEM((2 * HALO + 1, 16, total), F32),
            dma((8,)),
            dma,
            dma((2,)),
            dma((2 * chunks,)),
            dma((2 * chunks,)),
            dma((2 * HALO + 1,)),
            dma((2 * HALO + 1,)),
        ],
        compiler_params=pltpu.CompilerParams(
            collective_id=0, has_side_effects=True, vmem_limit_bytes=64_000_000
        ),
        name="exchange",
    )(*dft_tables(side), pair_list, pair_count, tissue, patches)
    return pl.pallas_call(
        relax,
        out_shape=(
            jax.ShapeDtypeStruct((1, 2, slots), F32),
            jax.ShapeDtypeStruct((1, 2, total), F32),
        ),
        in_specs=[vmem],
        out_specs=(vmem, vmem),
        name="relax",
    )(halo)


def solution(mesh):
    return jax.shard_map(
        functools.partial(on_device, mesh.shape["sec"]),
        mesh=mesh,
        in_specs=(
            P(("group", "sec"), None, None, None),
            P(("group", "sec"), None),
            P(("group", "sec")),
            P(("group", "sec"), None),
        ),
        out_specs=(P(("group", "sec"), None, None), P(("group", "sec"), None, None)),
        check_vma=False,
    )
```

```python
import functools

import jax
import jax.numpy as jnp
import numpy as np
from jax import lax
from jax.experimental import pallas as pl
from jax.experimental.pallas import tpu as pltpu
from jax.sharding import PartitionSpec as P

GR = 8
SPRING = 0.25
STEP = 0.15
CHUNK = 8
HALO = 3
MESH = pl.DeviceIdType.MESH
F32 = jnp.float32
BF16 = jnp.bfloat16


def dft_tables(length):
    index = np.arange(length)
    angle = (index[:, None] * index[None, :] % length) * (2.0 * np.pi / length)
    c = np.cos(angle).astype(np.float32)
    s = np.sin(angle).astype(np.float32)
    right = np.concatenate([c, s], axis=1)
    left = np.block([[c, -s], [-s, -c]])
    inner = np.block([[c, s], [-s, c]])
    last = np.concatenate([c, -s], axis=1)
    return tuple(jnp.asarray(t.astype(jnp.bfloat16)) for t in (right, left, inner, last))


def dot(a, b):
    return jnp.dot(a, b, preferred_element_type=F32)


def dot_nt(a, b):
    return lax.dot_general(a, b, (((1,), (1,)), ((), ())), preferred_element_type=F32)


def split3(x):
    top = x.astype(BF16)
    rest = x - top.astype(F32)
    mid = rest.astype(BF16)
    return top, mid, (rest - mid.astype(F32)).astype(BF16)


def stacked(both, a, b, side):
    ra = both[a * side : (a + 1) * side]
    rb = both[b * side : (b + 1) * side]
    top = jnp.concatenate([ra[:, :side], rb[:, :side]], axis=1)
    low = jnp.concatenate([ra[:, side:], rb[:, side:]], axis=1)
    return jnp.concatenate([top, low], axis=0)


def spectra(images, right, left):
    side = images[0].shape[0]
    rows = jnp.concatenate(images, axis=0)
    both = dot(rows, right).astype(BF16)
    return [dot(left, stacked(both, 2 * i, 2 * i + 1, side)) for i in range(len(images) // 2)]


def lane_roll(x, shift):
    return pltpu.roll(x, shift % x.shape[-1], x.ndim - 1)


def up_chunks(pair, n, chunks):
    return chunks * ((pair + 1) // 2) // (n // 2)


def exchange(
    n,
    right_any,
    left_any,
    inner_any,
    last_any,
    list_any,
    count_s,
    tissue_any,
    patches_any,
    out_ref,
    patches,
    right_ref,
    left_ref,
    inner_ref,
    last_ref,
    list_v,
    list_s,
    tissue_v,
    note,
    far_note,
    far_s,
    outgoing,
    incoming,
    own_spec,
    peak_ref,
    mass_ref,
    moment_ref,
    packet,
    halo,
    load_sems,
    smem_sem,
    list_sems,
    send_sems,
    recv_sems,
    halo_send,
    halo_recv,
):
    me = lax.axis_index("sec")
    total, side, _ = patches.shape
    slots = list_v.shape[1]
    chunks = slots // CHUNK
    offsets = [d * sign for d in range(HALO, 0, -1) for sign in (1, -1)]

    loads = [
        pltpu.make_async_copy(source, target, load_sems.at[i])
        for i, (source, target) in enumerate(
            (
                (list_any, list_v),
                (list_any, list_s),
                (patches_any.at[0], patches),
                (right_any, right_ref),
                (left_any, left_ref),
                (inner_any, inner_ref),
                (last_any, last_ref),
                (tissue_any, tissue_v),
            )
        )
    ]
    for load in loads:
        load.start()

    halo[...] = jnp.zeros_like(halo)
    far_note[...] = jnp.zeros_like(far_note)

    barrier = pltpu.get_barrier_semaphore()
    for d in offsets:

        @pl.when((me + d >= 0) & (me + d < n))
        def _():
            pl.semaphore_signal(barrier, inc=1, device_id={"sec": me + d}, device_id_type=MESH)

    for load in loads[:2]:
        load.wait()
    count = count_s[0]
    note[...] = jnp.concatenate([list_v[...], jnp.full((1, slots), count, jnp.int32)], axis=0)

    has_up = jnp.minimum(n - 1 - me, 1)
    has_down = jnp.minimum(me, 1)
    my_up = up_chunks(me, n, chunks)
    far_up = up_chunks(me - 1, n, chunks)

    pl.semaphore_wait(barrier, jnp.minimum(me, HALO) + jnp.minimum(n - 1 - me, HALO))

    list_copy = pltpu.make_async_remote_copy(
        src_ref=note,
        dst_ref=far_note,
        send_sem=list_sems.at[0],
        recv_sem=list_sems.at[1],
        device_id={"sec": me + 1},
        device_id_type=MESH,
    )

    @pl.when(me < n - 1)
    def _():
        list_copy.start()

    loads[2].wait()

    def patch_copy(q, to):
        return pltpu.make_async_remote_copy(
            src_ref=outgoing.at[pl.ds(q * CHUNK, CHUNK)],
            dst_ref=incoming.at[pl.ds(q * CHUNK, CHUNK)],
            send_sem=send_sems.at[q],
            recv_sem=recv_sems.at[q],
            device_id={"sec": to},
            device_id_type=MESH,
        )

    def send_up(c, carry):
        for j in range(CHUNK):
            outgoing[c * CHUNK + j] = patches[list_s[0, c * CHUNK + j]]
        patch_copy(c, me + 1).start()
        return carry

    lax.fori_loop(0, has_up * my_up, send_up, 0)
    peak_ref[...] = jnp.zeros_like(peak_ref)
    mass_ref[...] = jnp.ones_like(mass_ref)
    moment_ref[...] = jnp.zeros_like(moment_ref)
    for load in loads[3:]:
        load.wait()

    def own_group(q, carry):
        images = []
        for j in range(CHUNK):
            far = far_s[0, jnp.minimum(q, chunks - 1) * CHUNK + j]
            near = list_s[0, jnp.maximum(q - chunks, 0) * CHUNK + j]
            images.append(patches[jnp.where(q < chunks, far, near)])
        for i, spec in enumerate(spectra(images, right_ref[...], left_ref[...])):
            own_spec[q * (CHUNK // 2) + i] = spec.astype(BF16)
        return carry

    @pl.when(me > 0)
    def _():
        list_copy.wait_recv()

    to_smem = pltpu.make_async_copy(far_note, far_s, smem_sem)
    to_smem.start()
    to_smem.wait()

    def send_down(c, carry):
        for j in range(CHUNK):
            outgoing[slots + c * CHUNK + j] = patches[far_s[0, c * CHUNK + j]]
        patch_copy(chunks + c, me - 1).start()
        return carry

    lax.fori_loop(far_up, far_up + has_down * (chunks - far_up), send_down, 0)
    lax.fori_loop(chunks + my_up, chunks + my_up + has_up * (chunks - my_up), own_group, 0)
    lax.fori_loop(0, has_down * far_up, own_group, 0)

    half = side // 2
    row = lax.broadcasted_iota(jnp.int32, (side, 1), 0)
    row_lag = ((row + half) % side - half).astype(F32)
    scale = 64.0 / float(side * side * side * side)

    def match_group(t, carry):
        start_a, count_a, start_b = carry
        q = jnp.where(t < count_a, start_a + t, start_b + t - count_a)
        patch_copy(q, me).wait_recv()
        sign = jnp.where(q < chunks, -1.0, 1.0).astype(F32)
        images = [incoming[q * CHUNK + j] for j in range(CHUNK)]
        crosses = []
        for i, spec in enumerate(spectra(images, right_ref[...], left_ref[...])):
            ar = spec[:side].astype(BF16).astype(F32)
            ai = spec[side:].astype(BF16).astype(F32)
            own = own_spec[q * (CHUNK // 2) + i].astype(F32)
            br, bi = own[:side], own[side:]
            cr = (br * ar + bi * ai).astype(BF16)
            ci = ((br * ai - bi * ar) * sign).astype(BF16)
            crosses.append(jnp.concatenate([cr[:, :side], ci[:, :side]], axis=1))
            crosses.append(jnp.concatenate([cr[:, side:], ci[:, side:]], axis=1))
        inner = dot(jnp.concatenate(crosses, axis=0), inner_ref[...]).astype(BF16)
        peaks, masses, moments = [], [], []
        for i in range(CHUNK // 2):
            scores = dot(last_ref[...], stacked(inner, 2 * i, 2 * i + 1, side)) * scale
            peak = jnp.max(scores, axis=0, keepdims=True)
            e = jnp.exp(scores - peak)
            mass = jnp.sum(e, axis=0, keepdims=True)
            moment = jnp.sum(e * row_lag, axis=0, keepdims=True)
            for parts, value in ((peaks, peak), (masses, mass), (moments, moment)):
                parts.append(value[:, :side])
                parts.append(value[:, side:])
        at = pl.ds(pl.multiple_of(q * CHUNK, CHUNK), CHUNK)
        peak_ref[at, :] = jnp.concatenate(peaks, axis=0)
        mass_ref[at, :] = jnp.concatenate(masses, axis=0)
        moment_ref[at, :] = jnp.concatenate(moments, axis=0)
        return carry

    n_far = has_down * far_up
    n_near = has_up * (chunks - my_up)
    odd = me % 2
    start_a = (1 - odd) * (chunks + my_up)
    start_b = odd * (chunks + my_up)
    count_a = odd * n_far + (1 - odd) * n_near
    lax.fori_loop(0, n_far + n_near, match_group, (start_a, count_a, start_b))

    peak = peak_ref[...]
    weight = jnp.exp(peak - jnp.max(peak, axis=1, keepdims=True))
    mass = mass_ref[...] * weight
    moment = moment_ref[...] * weight
    col = lax.broadcasted_iota(jnp.int32, (8, side), 1)
    sub = lax.broadcasted_iota(jnp.int32, (8, side), 0)
    col_lag = ((col + half) % side - half).astype(F32)
    axes = jnp.where(sub == 0, 1.0, jnp.where(sub == 1, col_lag, 0.0))
    thirds = jnp.concatenate(split3(jnp.concatenate([mass, moment], axis=0)), axis=0)
    triple = dot_nt(axes.astype(BF16), thirds)
    span = 4 * slots
    joined = triple[:, 0:span] + triple[:, span : 2 * span] + triple[:, 2 * span :]
    sums, rows_num = joined[:, 0 : 2 * slots], joined[:, 2 * slots :]
    mass_all = sums[0:1]
    place = lax.broadcasted_iota(jnp.int32, (1, 2 * slots), 1)
    is_far = place < slots
    far = far_note[...]
    counts = jnp.concatenate([far[1:2], jnp.full((1, slots), count, jnp.int32)], axis=1)
    lists = jnp.concatenate([far[0:1], list_v[...]], axis=1)
    slot = jnp.where(is_far, place, place - slots)
    first = jnp.where(is_far, 0, (chunks - n_near) * CHUNK)
    stop = jnp.minimum(jnp.where(is_far, n_far * CHUNK, slots), counts)
    live = (slot >= first) & (slot < stop)
    flow_rows = jnp.where(live, rows_num[0:1] / mass_all, 0.0)
    flow_cols = jnp.where(live, sums[1:2] / mass_all, 0.0)
    which = lax.broadcasted_iota(jnp.int32, (total, 2 * slots), 0)
    onehot = (which == lists).astype(F32).astype(BF16)
    one_pair = jnp.concatenate(
        [flow_rows, flow_cols, live.astype(F32), jnp.zeros((5, 2 * slots), F32)], axis=0
    )
    both = jnp.concatenate(
        [jnp.where(is_far, one_pair, 0.0), jnp.where(is_far, 0.0, one_pair)], axis=0
    )
    triple = dot_nt(jnp.concatenate(split3(both), axis=0), onehot)
    field = triple[0:16] + triple[16:32] + triple[32:48]
    packet[0:3] = field[0:3]
    packet[3:4] = tissue_v[...].astype(F32)
    packet[4:8] = field[4:8]
    packet[8:16] = field[8:16]
    packet[4:5, 0 : 2 * slots] = flow_rows
    packet[5:6, 0 : 2 * slots] = flow_cols

    def halo_copy(d):
        return pltpu.make_async_remote_copy(
            src_ref=packet,
            dst_ref=halo.at[HALO - d],
            send_sem=halo_send.at[HALO - d],
            recv_sem=halo_recv.at[HALO - d],
            device_id={"sec": me + d},
            device_id_type=MESH,
        )

    for d in offsets:

        @pl.when((me + d >= 0) & (me + d < n))
        def _():
            halo_copy(d).start()

    for d in offsets:

        @pl.when((me - d >= 0) & (me - d < n))
        def _():
            halo_copy(d).wait_recv()

    @pl.when(me < n - 1)
    def _():
        list_copy.wait_send()

    def drain_up(c, carry):
        patch_copy(c, me + 1).wait_send()
        return carry

    lax.fori_loop(0, has_up * my_up, drain_up, 0)

    def drain_down(c, carry):
        patch_copy(chunks + c, me - 1).wait_send()
        return carry

    lax.fori_loop(far_up, far_up + has_down * (chunks - far_up), drain_down, 0)
    for d in offsets:
        out_ref[HALO + d] = halo[HALO + d]
    out_ref[HALO] = packet[...]
    for d in offsets:

        @pl.when((me + d >= 0) & (me + d < n))
        def _():
            halo_copy(d).wait_send()


def relax(halo, flow_ref, pos_ref):
    total = halo.shape[-1]
    slots = flow_ref.shape[-1]
    near, above = halo[HALO], halo[HALO + 1]
    flow_ref[0] = near[4:6, slots : 2 * slots] + above[4:6, 0:slots]
    fields = {d: halo[HALO + d][8:16] + halo[HALO + d + 1][0:8] for d in range(-HALO, HALO)}
    links = {d: jnp.broadcast_to(f[2:3], f.shape) for d, f in fields.items()}
    lane = lax.broadcasted_iota(jnp.int32, (8, total), 1)
    width = total // GR
    has_right = (lane % width) != width - 1
    has_below = lane < total - width

    def springs(d):
        tissue = jnp.broadcast_to(halo[HALO + d][3:4], (8, total))
        stiff = SPRING * (1.0 + 2.0 * tissue)
        across = jnp.where(has_right, 0.5 * (stiff + lane_roll(stiff, -1)), 0.0)
        along = jnp.where(has_below, 0.5 * (stiff + lane_roll(stiff, -width)), 0.0)
        return across, along

    def plane(u, spring):
        across, along = spring
        a = across * (lane_roll(u, -1) - u)
        b = along * (lane_roll(u, -width) - u)
        return (lane_roll(a, 1) - a) + (lane_roll(b, width) - b)

    spring = {d: springs(d) for d in (-1, 0, 1)}
    pull = {d: links[d] * fields[d] for d in fields}
    u1 = {d: -STEP * (pull[d] - pull[d - 1]) for d in range(-2, 3)}

    def relaxed(u, d):
        gap_here = u[d + 1] - u[d] - fields[d]
        gap_below = u[d] - u[d - 1] - fields[d - 1]
        force = plane(u[d], spring[d]) - links[d] * gap_here + links[d - 1] * gap_below
        return u[d] - STEP * force

    u2 = {d: relaxed(u1, d) for d in (-1, 0, 1)}
    pos_ref[0] = relaxed(u2, 0)[0:2]


def on_device(n, patches, pair_list, pair_count, tissue):
    _, total, side, _ = patches.shape
    slots = pair_list.shape[1]
    chunks = slots // CHUNK
    vmem = pl.BlockSpec(memory_space=pltpu.VMEM)
    any_space = pl.BlockSpec(memory_space=pl.ANY)
    dma = pltpu.SemaphoreType.DMA
    halo = pl.pallas_call(
        functools.partial(exchange, n),
        out_shape=jax.ShapeDtypeStruct((2 * HALO + 1, 16, total), F32),
        in_specs=[any_space] * 5 + [pl.BlockSpec(memory_space=pltpu.SMEM)] + [any_space] * 2,
        out_specs=vmem,
        scratch_shapes=[
            pltpu.VMEM((total, side, side), BF16),
            pltpu.VMEM((side, 2 * side), BF16),
            pltpu.VMEM((2 * side, 2 * side), BF16),
            pltpu.VMEM((2 * side, 2 * side), BF16),
            pltpu.VMEM((side, 2 * side), BF16),
            pltpu.VMEM((1, slots), jnp.int32),
            pltpu.SMEM((1, slots), jnp.int32),
            pltpu.VMEM((1, total), jnp.int32),
            pltpu.VMEM((2, slots), jnp.int32),
            pltpu.VMEM((2, slots), jnp.int32),
            pltpu.SMEM((2, slots), jnp.int32),
            pltpu.VMEM((2 * slots, side, side), BF16),
            pltpu.VMEM((2 * slots, side, side), BF16),
            pltpu.VMEM((slots, 2 * side, 2 * side), BF16),
            pltpu.VMEM((2 * slots, side), F32),
            pltpu.VMEM((2 * slots, side), F32),
            pltpu.VMEM((2 * slots, side), F32),
            pltpu.VMEM((16, total), F32),
            pltpu.VMEM((2 * HALO + 1, 16, total), F32),
            dma((8,)),
            dma,
            dma((2,)),
            dma((2 * chunks,)),
            dma((2 * chunks,)),
            dma((2 * HALO + 1,)),
            dma((2 * HALO + 1,)),
        ],
        compiler_params=pltpu.CompilerParams(
            collective_id=0, has_side_effects=True, vmem_limit_bytes=64_000_000
        ),
        name="exchange",
    )(*dft_tables(side), pair_list, pair_count, tissue, patches)
    return pl.pallas_call(
        relax,
        out_shape=(
            jax.ShapeDtypeStruct((1, 2, slots), F32),
            jax.ShapeDtypeStruct((1, 2, total), F32),
        ),
        in_specs=[vmem],
        out_specs=(vmem, vmem),
        name="relax",
    )(halo)


def solution(mesh):
    return jax.shard_map(
        functools.partial(on_device, mesh.shape["sec"]),
        mesh=mesh,
        in_specs=(
            P(("group", "sec"), None, None, None),
            P(("group", "sec"), None),
            P(("group", "sec")),
            P(("group", "sec"), None),
        ),
        out_specs=(P(("group", "sec"), None, None), P(("group", "sec"), None, None)),
        check_vma=False,
    )
```
